256 devices in a mesh: lat: 8 (over z_hi, core), lon: 32 (over x, z_lo, y).
Axes of the slice: x: 4, y: 4, z: 8 (z_hi: 4, z_lo: 2; z = z_hi * 2 + z_lo), core: 2. Of those that a mesh axis runs over, the one named last changes fastest.
Arguments:
- forcing: bfloat16 [16, 128, 4096], P(None, 'lat', 'lon'), may hold values from -6 to 6
- hidden: bfloat16 [64, 128, 4096], P(None, 'lat', 'lon'), may hold values from -3 to 3
- cell: bfloat16 [64, 128, 4096], P(None, 'lat', 'lon'), may hold values from -6 to 6
- grad_hidden: bfloat16 [64, 128, 4096], P(None, 'lat', 'lon'), may hold values from -6 to 6
- grad_cell: bfloat16 [64, 128, 4096], P(None, 'lat', 'lon'), may hold values from -6 to 6
- wet_mask: int32 [8, 256], P('lat'), may hold values from 0 to 1
- tile_owner: int32 [8, 256], P('lat'), may hold values from 0 to 31, as said below
- w_gates: bfloat16 [256, 720], replicated, may hold values from -0.21875 to 0.21875
- b_gates: float32 [256], replicated, may hold values from -3 to 3
Outputs:
- hidden_next: bfloat16 [64, 128, 4096], P(None, 'lat', 'lon')
- cell_next: float32 [1024, 64, 256], P(('lat', 'lon'))
- hidden_grad: float32 [64, 128, 4096], P(None, 'lat', 'lon')
- cell_grad: float32 [64, 128, 4096], P(None, 'lat', 'lon')
- weight_grad: float32 [256, 720], replicated
- bias_grad: float32 [256], replicated
The draws below stay inside these ranges and needn't reach their ends.
Inputs may be any that keep to these rules, and one draw needn't show every extreme that they name: Within each group of 1 tile rows, tile_owner gives every longitude index exactly 4 wet tiles, and gives the wet tiles of one longitude block of 8 tile columns at most 1 to any one index; both bounds are reached in every draw, and some block is wet throughout. Dry tiles carry an owner too.
All inputs are finite; a program needn't handle non-finite values.
Results may differ from the reference program's by a relative error of at most 0.0033.
Values may be sent and summed in bfloat16 or wider, within the bound.
A program may use at most 64 MiB of HBM per device.

```python
import jax
import jax.numpy as jnp
from jax import lax

TILE = 16
INP = 16
HID = 64
TLAT_DEV = 1
TLON_DEV = 8
GATES = 256
CH = 80
TD = 8
CAP = 4
NTLAT = 8
NTLON = 256
NLAT = 128
NLON = 4096
WORK = 1024
N_LAT = 8
N_LON = 32


def tile_layout(key):
    groups = NTLAT // TLAT_DEV
    device_total = NTLON // TLON_DEV
    per_dev = TLAT_DEV * TLON_DEV
    length_count = device_total * per_dev
    wet_total = CAP * device_total

    def one_group(cluster_key):
        boost_key, jitter_key, shuffle_key, offset_key, landmask_key = jax.random.split(cluster_key, 5)
        device_boost = jax.random.randint(boost_key, (device_total,), 0, 4 * length_count)
        unique_owners = device_boost * device_total + jnp.arange(device_total, dtype=jnp.int32)
        best_device = lax.top_k(unique_owners, 1)[1][0]
        device_boost = device_boost + jnp.where(jnp.arange(device_total, dtype=jnp.int32) == best_device, 100 * length_count, 0)
        tile_jitter = jax.random.randint(jitter_key, (device_total, per_dev), 0, 2 * length_count)
        tile_rating = ((tile_jitter + device_boost[:, None]) * length_count).reshape(length_count) + jnp.arange(length_count, dtype=jnp.int32)
        chosen = lax.top_k(tile_rating, wet_total)[1]
        wet_flag = jnp.zeros((length_count,), jnp.int32).at[chosen].set(1)
        wet_rank = jnp.cumsum(wet_flag) - 1
        labels = jax.random.permutation(shuffle_key, device_total).astype(jnp.int32)
        label_shift = jax.random.randint(offset_key, (), 0, device_total)
        wet_owner = labels[(wet_rank + label_shift) % device_total]
        dry_owner = jax.random.randint(landmask_key, (length_count,), 0, device_total)
        owner_flag = jnp.where(wet_flag > 0, wet_owner, dry_owner).astype(jnp.int32)
        return (wet_flag, owner_flag)
    group_keys = jax.random.split(jax.random.fold_in(key, 11), groups)
    wet_flag, owner_flag = jax.vmap(one_group)(group_keys)

    def to_grid(values):
        return values.reshape(groups, device_total, TLAT_DEV, TLON_DEV).transpose(0, 2, 1, 3).reshape(NTLAT, NTLON)
    return (to_grid(wet_flag), to_grid(owner_flag))


def draw_wet_mask(key, part):
    return tile_layout(key)[0]


def draw_tile_owner(key, part):
    return tile_layout(key)[1]


def block_scale(stream_key, extent, cuts, low, top_value):
    factor_of, own = 1.0, jax.random.fold_in(stream_key, 6)
    for dim, parts in cuts:
        steps = jnp.exp(jax.random.uniform(jax.random.fold_in(own, dim), (parts,), jnp.float32, low / len(cuts), top_value / len(cuts)))
        factor_of = factor_of * jnp.repeat(steps, extent[dim] // parts).reshape([-1 if axis == dim else 1 for axis in range(len(extent))])
    return factor_of


def bell_draw(rng, shape, scale, most, cuts=(), kind=jnp.bfloat16):
    gain = block_scale(rng, shape, cuts, -0.22, 0.18) if cuts else 1.0
    entries = jax.random.normal(rng, shape, jnp.float32) * scale * gain
    return jnp.minimum(jnp.maximum(entries, -most), most).astype(kind)


def setup_inputs(seed: int = 0) -> dict:
    key_of = jax.random.split(jax.random.key(seed), 10)
    return {
        "forcing": bell_draw(key_of[0], (INP, NLAT, NLON), 1.0, 6.0, ((1, 8), (2, 32))),
        "hidden": bell_draw(key_of[1], (HID, NLAT, NLON), 0.5, 3.0, ((1, 8), (2, 32))),
        "cell": bell_draw(key_of[2], (HID, NLAT, NLON), 1.0, 6.0, ((1, 8), (2, 32))),
        "grad_hidden": bell_draw(key_of[3], (HID, NLAT, NLON), 1.0, 6.0, ((1, 8), (2, 32))),
        "grad_cell": bell_draw(key_of[4], (HID, NLAT, NLON), 1.0, 6.0, ((1, 8), (2, 32))),
        "wet_mask": draw_wet_mask(jax.random.fold_in(key_of[9], 71), 0),
        "tile_owner": draw_tile_owner(jax.random.fold_in(key_of[9], 71), 0),
        "w_gates": bell_draw(key_of[7], (GATES, 9 * CH), (9 * CH) ** -0.5, 0.21875),
        "b_gates": bell_draw(key_of[8], (GATES,), 0.5, 3.0, (), jnp.float32),
    }


def last_pad(values_in, pad_front, pad_back):
    widths = [(0, 0)] * (values_in.ndim - 1) + [(pad_front, pad_back)]
    return jnp.pad(values_in, widths)

def fold_edges(values_in):
    tile_count = values_in.shape[-2]
    inner_size = values_in.shape[-1] - 2
    leading = values_in.shape[:-2]
    flat_shape = leading + (tile_count * inner_size,)
    middle = values_in[..., 1:inner_size + 1].reshape(flat_shape)
    zeros_left = jnp.zeros(leading + (tile_count, inner_size - 1), values_in.dtype)
    left_edge = jnp.concatenate([values_in[..., 0:1], zeros_left], -1).reshape(flat_shape)
    zeros_one = jnp.zeros(leading + (tile_count, 1), values_in.dtype)
    zeros_rest = jnp.zeros(leading + (tile_count, inner_size - 2), values_in.dtype)
    right_edge = jnp.concatenate([zeros_one, values_in[..., inner_size + 1:inner_size + 2], zeros_rest], -1).reshape(flat_shape)
    full_size = tile_count * inner_size + 2
    return last_pad(middle, 1, 1) + last_pad(left_edge, 0, 2) + last_pad(right_edge, inner_size, 0)[..., :full_size]

def lstm_terms(pre_in, pre_forget, pre_out, pre_cand, cell_in, hidden_cot, cell_cot, live_cells):
    gate_in = jax.nn.sigmoid(pre_in)
    gate_forget = jax.nn.sigmoid(pre_forget)
    gate_out = jax.nn.sigmoid(pre_out)
    candidate = jnp.tanh(pre_cand)
    cell_new = gate_forget * cell_in + gate_in * candidate
    squash = jnp.tanh(cell_new)
    hidden_new = (live_cells * gate_out * squash).astype(jnp.bfloat16)
    back_h = live_cells * hidden_cot.astype(jnp.float32)
    back_c = live_cells * cell_cot.astype(jnp.float32) + back_h * gate_out * (1.0 - squash * squash)
    cell_back = back_c * gate_forget
    delta_parts = (back_c * candidate * gate_in * (1.0 - gate_in), back_c * cell_in * gate_forget * (1.0 - gate_forget), back_h * squash * gate_out * (1.0 - gate_out), back_c * gate_in * (1.0 - candidate * candidate))
    return (hidden_new, cell_new, cell_back, delta_parts)

def gate_block(slab_in, cell_blk, hidden_cot, cell_cot, live_row, w_gates, b_gates):
    channels = slab_in.shape[0]
    hid_count = cell_blk.shape[0]
    row_count = cell_blk.shape[1]
    lon_count = cell_blk.shape[2]
    cells = row_count * lon_count
    tap_list = []
    for row_off in range(3):
        for col_off in range(3):
            tap_list.append(slab_in[:, row_off:row_off + row_count, col_off:col_off + lon_count].reshape(channels, cells))
    patches = jnp.concatenate(tap_list, 0).astype(jnp.float32)
    weights = w_gates.astype(jnp.float32)
    pre_gates = jnp.dot(weights, patches, preferred_element_type=jnp.float32, precision=lax.Precision.HIGHEST) + b_gates[:, None]
    live_cells = jnp.tile(live_row, row_count)[None, :]
    hidden_new, cell_new, cell_back, delta_parts = lstm_terms(pre_gates[:hid_count], pre_gates[hid_count:2 * hid_count], pre_gates[2 * hid_count:3 * hid_count], pre_gates[3 * hid_count:], cell_blk.reshape(hid_count, cells).astype(jnp.float32), hidden_cot.reshape(hid_count, cells), cell_cot.reshape(hid_count, cells), live_cells)
    gate_delta = lax.optimization_barrier(jnp.concatenate(delta_parts, 0).astype(jnp.bfloat16)).astype(jnp.float32)
    weight_part = jnp.dot(gate_delta, patches.T, preferred_element_type=jnp.float32, precision=lax.Precision.HIGHEST)
    bias_part = lax.optimization_barrier(jnp.sum(gate_delta, 1))
    hid_weights = weights.reshape(weights.shape[0], 9, channels)[:, :, channels - hid_count:]
    spread = jnp.einsum('gth,gc->thc', hid_weights, gate_delta, precision=lax.Precision.HIGHEST)
    grad_pad = jnp.zeros((hid_count, row_count + 2, lon_count + 2), jnp.float32)
    for row_off in range(3):
        for col_off in range(3):
            placed = spread[row_off * 3 + col_off].reshape(hid_count, row_count, lon_count)
            grad_pad = grad_pad + jnp.pad(placed, ((0, 0), (row_off, 2 - row_off), (col_off, 2 - col_off)))
    shape_out = (hid_count, row_count, lon_count)
    return (hidden_new.reshape(shape_out), cell_new.reshape(shape_out), cell_back.reshape(shape_out), grad_pad, weight_part, bias_part)

def reference(forcing, hidden, cell, grad_hidden, grad_cell, wet_mask, tile_owner, w_gates, b_gates):
    fields = jnp.concatenate([forcing, hidden], 0)
    wrapped = jnp.concatenate([fields[:, :, -1:], fields, fields[:, :, :1]], 2)
    padded = jnp.pad(wrapped, ((0, 0), (1, 1), (0, 0)))
    live_rows = jnp.repeat(wet_mask.astype(jnp.float32), TILE, axis=1)

    def scan_step(carry, block_row):
        top_row = (block_row * TILE).astype(jnp.int32)
        slab_in = lax.dynamic_slice_in_dim(padded, top_row, TILE + 2, 1)
        cell_blk = lax.dynamic_slice_in_dim(cell, top_row, TILE, 1)
        hidden_cot = lax.dynamic_slice_in_dim(grad_hidden, top_row, TILE, 1)
        cell_cot = lax.dynamic_slice_in_dim(grad_cell, top_row, TILE, 1)
        live_row = live_rows[block_row]
        results = gate_block(slab_in, cell_blk, hidden_cot, cell_cot, live_row, w_gates, b_gates)
        return ((carry[0] + results[4], carry[1] + results[5]), results[:4])
    start_sums = (jnp.zeros((GATES, 9 * CH), jnp.float32), jnp.zeros((GATES,), jnp.float32))
    totals, stacked = lax.scan(scan_step, start_sums, jnp.arange(NTLAT, dtype=jnp.int32))
    hid_blocks, cell_blocks, back_blocks, pad_blocks = stacked

    def merge_rows(blocks):
        return jnp.moveaxis(blocks, 0, 1).reshape(HID, NLAT, NLON)
    hidden_next = merge_rows(hid_blocks)
    cell_grad = merge_rows(back_blocks)
    lon_fold = pad_blocks[..., 1:NLON + 1]
    lon_fold = lon_fold.at[..., NLON - 1].add(pad_blocks[..., 0])
    lon_fold = lon_fold.at[..., 0].add(pad_blocks[..., NLON + 1])
    lat_major = jnp.transpose(lon_fold, (1, 3, 0, 2))
    hidden_grad = jnp.transpose(fold_edges(lat_major)[..., 1:NLAT + 1], (0, 2, 1))
    scaling = 1.0 / jnp.sqrt(jnp.float32(WORK * TILE * TILE))
    weight_grad = totals[0] * scaling
    bias_grad = totals[1] * scaling
    cell_grid = merge_rows(cell_blocks)
    cell_tiles = cell_grid.reshape(HID, NTLAT, TILE, NTLON, TILE).transpose(1, 3, 0, 2, 4).reshape(NTLAT * NTLON, HID, TILE * TILE)
    wet_order = wet_mask.reshape(N_LAT, TLAT_DEV, N_LON, TLON_DEV).transpose(0, 2, 1, 3).reshape(N_LAT, N_LON * TD)
    owner_order = tile_owner.reshape(N_LAT, TLAT_DEV, N_LON, TLON_DEV).transpose(0, 2, 1, 3).reshape(N_LAT, N_LON * TD)
    owner_hits = ((wet_order[..., None] > 0) & (owner_order[..., None] == jnp.arange(N_LON, dtype=jnp.int32)[None, None, :])).astype(jnp.int32)
    before = jnp.cumsum(owner_hits, 1) - owner_hits
    owner_rank = lax.optimization_barrier(jnp.sum(before * owner_hits, -1))
    group_index = jnp.arange(N_LAT, dtype=jnp.int32)[:, None]
    target = jnp.where(wet_order > 0, (group_index * N_LON + owner_order) * CAP + owner_rank, WORK).astype(jnp.int32)
    target = target.reshape(N_LAT, N_LON, TLAT_DEV, TLON_DEV).transpose(0, 2, 1, 3).reshape(NTLAT * NTLON)
    cell_next = jnp.zeros((WORK + 1, HID, TILE * TILE), jnp.float32).at[target].set(cell_tiles)[:WORK]
    return (hidden_next, cell_next, hidden_grad, cell_grad, weight_grad, bias_grad)
```

```python
import functools
import math

import jax
import jax.numpy as jnp
from jax import lax
from jax.experimental import pallas as pl
from jax.experimental.pallas import tpu as pltpu
from jax.sharding import PartitionSpec as P

MESH = pl.DeviceIdType.MESH
F32 = jnp.float32
BF16 = jnp.bfloat16
ROWS = 16
LANES = 128
INP = 16
HID = 64
CH = 80
GATES = 256
TAP3 = 240
CAP = 4
TILES = 8
HALF = 384


def lane_iota(rows):
    return lax.broadcasted_iota(jnp.int32, (rows, LANES), 1)


def row_of(i):
    return pl.ds(pl.multiple_of(i * LANES, LANES), LANES)


def sigmoid(x):
    return 0.5 * jnp.tanh(0.5 * x) + 0.5


def step_kernel(
    nlat,
    nlon,
    forcing,
    hidden,
    cell,
    grad_h,
    grad_c,
    wet,
    owner,
    w_ref,
    b_ref,
    hid_o,
    cg_o,
    cn_o,
    hg_o,
    ge_o,
    ag_o,
    f32f,
    f32h,
    f32c,
    f32gh,
    f32gc,
    hid32,
    e,
    wp,
    wt,
    bcol,
    delta,
    crow,
    tiles,
    slots,
    recv,
    g32,
    wgs,
    rsr,
    las,
    lar,
    ags,
    hs,
    hr,
    gs,
    h_send,
    h_recv,
    g_send,
    g_recv,
    a_send,
    a_recv,
    r_send,
    r_recv,
    l_send,
    l_recv,
    q_send,
    q_recv,
    slot_tab,
    work_tab,
):
    lat = lax.axis_index("lat")
    lon = lax.axis_index("lon")
    up = lax.rem(lat + nlat - 1, nlat)
    down = lax.rem(lat + 1, nlat)
    left = lax.rem(lon + nlon - 1, nlon)
    right = lax.rem(lon + 1, nlon)

    def lon_peer(k):
        return lax.rem(lon + k, nlon)

    def lat_peer(k):
        return lax.rem(lat + k, nlat)

    diagonals = ((up, left), (up, right), (down, left), (down, right))

    barrier = pltpu.get_barrier_semaphore()
    for place in diagonals:
        pl.semaphore_signal(barrier, inc=1, device_id=place, device_id_type=MESH)

    def greet_lat(k, c):
        pl.semaphore_signal(barrier, inc=1, device_id=(lat_peer(k), lon), device_id_type=MESH)
        return c

    lax.fori_loop(1, nlat, greet_lat, 0)

    def greet_lon(k, c):
        pl.semaphore_signal(barrier, inc=1, device_id=(lat, lon_peer(k)), device_id_type=MESH)
        return c

    lax.fori_loop(1, nlon, greet_lon, 0)

    f32f[...] = forcing[...].astype(F32).reshape(INP * ROWS, LANES)
    f32h[...] = hidden[...].astype(F32).reshape(HID * ROWS, LANES)
    lane80 = lane_iota(CH)

    def field_row(i):
        return jnp.concatenate(
            [f32f[pl.ds(i, INP, stride=ROWS), :], f32h[pl.ds(i, HID, stride=ROWS), :]], 0
        )

    edge_l = jnp.zeros((CH, LANES), F32)
    edge_r = jnp.zeros((CH, LANES), F32)
    for i in range(ROWS):
        row = field_row(i)
        e[CH : 2 * CH, (i + 1) * LANES : (i + 2) * LANES] = row.astype(BF16)
        e[0:CH, (i + 1) * LANES : (i + 2) * LANES] = pltpu.roll(row, 1, 1).astype(BF16)
        e[2 * CH : TAP3, (i + 1) * LANES : (i + 2) * LANES] = pltpu.roll(
            row, LANES - 1, 1
        ).astype(BF16)
        edge_l = jnp.where(lane80 == i, row[:, 0:1], edge_l)
        edge_r = jnp.where(lane80 == i, row[:, LANES - 1 : LANES], edge_r)
        if i == 0:
            hs[0] = row.astype(BF16)
        if i == ROWS - 1:
            hs[1] = row.astype(BF16)
    hs[2] = edge_l.astype(BF16)
    hs[3] = edge_r.astype(BF16)

    pl.semaphore_wait(barrier, nlon - 1 + nlat - 1 + 4)

    halo_plan = (
        (1, 0, (down, lon)),
        (0, 1, (up, lon)),
        (3, 2, (lat, right)),
        (2, 3, (lat, left)),
        (1, 4, (down, right)),
        (1, 5, (down, left)),
        (0, 6, (up, right)),
        (0, 7, (up, left)),
    )
    halo = []
    for src, dst, place in halo_plan:
        copy = pltpu.make_async_remote_copy(
            src_ref=hs.at[src],
            dst_ref=hr.at[dst],
            send_sem=h_send.at[dst],
            recv_sem=h_recv.at[dst],
            device_id=place,
            device_id_type=MESH,
        )
        copy.start()
        halo.append(copy)

    f32c[...] = cell[...].astype(F32).reshape(HID * ROWS, LANES)
    f32gh[...] = grad_h[...].astype(F32).reshape(HID * ROWS, LANES)
    f32gc[...] = grad_c[...].astype(F32).reshape(HID * ROWS, LANES)
    lane256 = lax.broadcasted_iota(jnp.int32, (GATES, GATES), 1)
    w_all = jnp.concatenate(
        [w_ref[...].astype(F32), jnp.zeros((GATES, 3 * GATES - 3 * TAP3), F32)], 1
    )
    for dr in range(3):
        part = w_all if dr == 0 else pltpu.roll(w_all, 3 * GATES - dr * TAP3, 1)
        part = jnp.where(lane256 < TAP3, part[:, :GATES], 0.0)
        wp[dr] = part.astype(BF16)
        wt[dr] = part.T.astype(BF16)
    bcol[...] = jnp.broadcast_to(b_ref[...], (LANES, GATES)).T
    ones_row = lax.broadcasted_iota(jnp.int32, (GATES - TAP3, 18 * LANES), 0) == 0
    e[TAP3:GATES, :] = jnp.where(ones_row, 1.0, 0.0).astype(BF16)
    delta[:, 0 : 2 * LANES] = jnp.zeros((GATES, 2 * LANES), BF16)
    delta[:, 18 * LANES : 20 * LANES] = jnp.zeros((GATES, 2 * LANES), BF16)

    base = lon * TILES
    wet_here = [wet[0, base + q] for q in range(TILES)]
    own_here = [owner[0, base + q] for q in range(TILES)]

    def plan_slot(o, c):
        source = jnp.int32(0)
        for q in range(TILES):
            source = source + jnp.where((wet_here[q] > 0) & (own_here[q] == o), q, 0)
        slot_tab[o] = source
        return c

    lax.fori_loop(0, nlon, plan_slot, 0)

    def plan_work(d, carry):
        count, work = carry
        has = jnp.int32(0)
        for q in range(TILES):
            has = has + jnp.where(
                (wet[0, d * TILES + q] > 0) & (owner[0, d * TILES + q] == lon), 1, 0
            )
        work = tuple(
            work[r] + jnp.where((has > 0) & (count == r), d, 0) for r in range(CAP)
        )
        return (count + has, work)

    _, work = lax.fori_loop(
        0, nlon, plan_work, (jnp.int32(0), tuple(jnp.int32(0) for _ in range(CAP)))
    )
    for r in range(CAP):
        work_tab[r] = work[r]

    lane64 = lane_iota(HID)
    live = jnp.zeros((HID, LANES), F32)
    for q in range(TILES):
        live = jnp.where(
            lane64 // 16 == q, jnp.where(wet_here[q] > 0, 1.0, 0.0).astype(F32), live
        )

    for copy in halo:
        copy.wait()

    keep_up = jnp.where(lat > 0, 1.0, 0.0).astype(F32)
    keep_down = jnp.where(lat < nlat - 1, 1.0, 0.0).astype(F32)
    from_left = hr[2].astype(F32)
    from_right = hr[3].astype(F32)
    for i in range(ROWS):
        cols = slice((i + 1) * LANES, (i + 2) * LANES)
        a = e[0:CH, cols].astype(F32)
        e[0:CH, cols] = jnp.where(
            lane80 == 0, pltpu.roll(from_left, (LANES - i) % LANES, 1), a
        ).astype(BF16)
        a = e[2 * CH : TAP3, cols].astype(F32)
        e[2 * CH : TAP3, cols] = jnp.where(
            lane80 == LANES - 1, pltpu.roll(from_right, LANES - 1 - i, 1), a
        ).astype(BF16)
    for block, keep, mid, lft, rgt in ((0, keep_up, 0, 4, 5), (17, keep_down, 1, 6, 7)):
        cols = slice(block * LANES, (block + 1) * LANES)
        row = hr[mid].astype(F32)
        e[CH : 2 * CH, cols] = (row * keep).astype(BF16)
        a = jnp.where(
            lane80 == 0, pltpu.roll(hr[lft].astype(F32), 1, 1), pltpu.roll(row, 1, 1)
        )
        e[0:CH, cols] = (a * keep).astype(BF16)
        a = jnp.where(
            lane80 == LANES - 1,
            pltpu.roll(hr[rgt].astype(F32), LANES - 1, 1),
            pltpu.roll(row, LANES - 1, 1),
        )
        e[2 * CH : TAP3, cols] = (a * keep).astype(BF16)

    def forward(c, carry):
        pre = jnp.zeros((GATES, 2 * LANES), F32)
        for dr in range(3):
            cols = pl.ds(pl.multiple_of(c * 2 * LANES + dr * LANES, LANES), 2 * LANES)
            pre = pre + jnp.dot(wp[dr], e[:, cols], preferred_element_type=F32)
        for s in range(2):
            i = c * 2 + s
            full = pre[:, s * LANES : (s + 1) * LANES] + bcol[...]
            g_in = sigmoid(full[0:HID])
            g_forget = sigmoid(full[HID : 2 * HID])
            g_out = sigmoid(full[2 * HID : 3 * HID])
            cand = jnp.tanh(full[3 * HID :])
            old = f32c[pl.ds(i, HID, stride=ROWS), :]
            new = g_forget * old + g_in * cand
            squash = jnp.tanh(new)
            crow[i] = new
            hid32[pl.ds(i, HID, stride=ROWS), :] = live * g_out * squash
            back_h = live * f32gh[pl.ds(i, HID, stride=ROWS), :]
            back_c = live * f32gc[pl.ds(i, HID, stride=ROWS), :] + back_h * g_out * (
                1.0 - squash * squash
            )
            cell_back = back_c * g_forget
            cg_o[pl.ds(i, HID, stride=ROWS), :] = cell_back
            back_in = back_c * g_in
            cols = row_of(i + 2)
            delta[0:HID, cols] = (back_in * cand * (1.0 - g_in)).astype(BF16)
            delta[HID : 2 * HID, cols] = (cell_back * old * (1.0 - g_forget)).astype(BF16)
            delta[2 * HID : 3 * HID, cols] = (
                back_h * squash * g_out * (1.0 - g_out)
            ).astype(BF16)
            delta[3 * HID :, cols] = (back_in * (1.0 - cand * cand)).astype(BF16)
        return carry

    lax.fori_loop(0, ROWS // 2, forward, 0)

    lane16 = lane_iota(16) // 16

    def regroup(step, carry):
        half = step // 4
        subs = pl.ds(pl.multiple_of(lax.rem(step, 4) * 16, 16), 16)
        x = [crow[half * 8 + k, subs, :] for k in range(8)]
        for s in (1, 2, 4):
            low = (lane16 // s) % 2 == 0
            y = list(x)
            for k in range(8):
                if (k // s) % 2 == 0:
                    a, b = x[k], x[k + s]
                    y[k] = jnp.where(low, a, pltpu.roll(b, 16 * s, 1))
                    y[k + s] = jnp.where(low, pltpu.roll(a, LANES - 16 * s, 1), b)
            x = y
        for q in range(8):
            tiles[q, subs, row_of(half)] = x[q].astype(BF16)
        return carry

    lax.fori_loop(0, 8, regroup, 0)

    def fill(o, carry):
        slots[o] = tiles[slot_tab[o]]
        return carry

    lax.fori_loop(0, nlon, fill, 0)
    recv[lon] = slots[lon]

    def tile_copy(k):
        peer = lon_peer(k)
        return pltpu.make_async_remote_copy(
            src_ref=slots.at[peer],
            dst_ref=recv.at[lon],
            send_sem=a_send.at[k],
            recv_sem=a_recv.at[k],
            device_id=(lat, peer),
            device_id_type=MESH,
        )

    def start_tile(k, c):
        tile_copy(k).start()
        return c

    for dr in range(3):
        g32[:, dr * GATES : (dr + 1) * GATES] = lax.dot_general(
            delta[:, 2 * LANES : 18 * LANES],
            e[:, dr * LANES : (dr + ROWS) * LANES],
            (((1,), (1,)), ((), ())),
            preferred_element_type=F32,
        )
    per = GATES // nlon

    def pack_terms(k, carry):
        rows = pl.ds(pl.multiple_of(k * per, per), per)
        wgs[k] = jnp.concatenate([g32[rows, :HALF], g32[rows, HALF:]], 0).astype(BF16)
        return carry

    lax.fori_loop(0, nlon, pack_terms, 0)
    rsr[lon] = wgs[lon]

    def scatter_copy(k):
        peer = lon_peer(k)
        return pltpu.make_async_remote_copy(
            src_ref=wgs.at[peer],
            dst_ref=rsr.at[lon],
            send_sem=r_send.at[k],
            recv_sem=r_recv.at[k],
            device_id=(lat, peer),
            device_id_type=MESH,
        )

    def start_scatter(k, c):
        scatter_copy(k).start()
        return c

    lax.fori_loop(1, nlon, start_scatter, 0)
    lax.fori_loop(1, nlon, start_tile, 0)

    colv_l = jnp.zeros((HID, LANES), F32)
    colv_r = jnp.zeros((HID, LANES), F32)
    for c in range(9):
        acc = jnp.zeros((GATES, 2 * LANES), F32)
        for dr in range(3):
            start = (2 * c + 2 - dr) * LANES
            acc = acc + jnp.dot(
                wt[dr], delta[:, start : start + 2 * LANES], preferred_element_type=F32
            )
        for s in range(2):
            r = 2 * c + s
            part = acc[:, s * LANES : (s + 1) * LANES]
            s0 = part[INP:CH]
            s1 = part[CH + INP : 2 * CH]
            s2 = part[2 * CH + INP : TAP3]
            colv_l = jnp.where(lane64 == r, s0[:, 0:1], colv_l)
            colv_r = jnp.where(lane64 == r, s2[:, LANES - 1 : LANES], colv_r)
            total = (
                s1
                + jnp.where(lane64 < LANES - 1, pltpu.roll(s0, LANES - 1, 1), 0.0)
                + jnp.where(lane64 > 0, pltpu.roll(s2, 1, 1), 0.0)
            )
            if r == 0:
                gs[0] = total.astype(BF16)
            elif r == 17:
                gs[1] = total.astype(BF16)
            else:
                hg_o[r - 1] = total
    gs[2] = colv_l.astype(BF16)
    gs[3] = colv_r.astype(BF16)
    grad_plan = (
        (1, 0, (down, lon)),
        (0, 1, (up, lon)),
        (3, 2, (lat, right)),
        (2, 3, (lat, left)),
        (3, 4, (down, right)),
        (2, 5, (down, left)),
        (3, 6, (up, right)),
        (2, 7, (up, left)),
    )
    edges = []
    for src, dst, place in grad_plan:
        copy = pltpu.make_async_remote_copy(
            src_ref=gs.at[src],
            dst_ref=ge_o.at[dst],
            send_sem=g_send.at[dst],
            recv_sem=g_recv.at[dst],
            device_id=place,
            device_id_type=MESH,
        )
        copy.start()
        edges.append(copy)
    hid_o[...] = hid32[...].reshape(HID, ROWS, LANES).astype(BF16)

    def wait_scatter(k, c):
        scatter_copy(k).wait()
        return c

    lax.fori_loop(1, nlon, wait_scatter, 0)
    lon_sum = lax.fori_loop(
        0, nlon, lambda k, t: t + rsr[k].astype(F32), jnp.zeros((2 * per, HALF), F32)
    )
    las[...] = lon_sum
    lar[lat] = lon_sum

    def lat_copy(k):
        peer = lat_peer(k)
        return pltpu.make_async_remote_copy(
            src_ref=las,
            dst_ref=lar.at[lat],
            send_sem=l_send.at[k],
            recv_sem=l_recv.at[k],
            device_id=(peer, lon),
            device_id_type=MESH,
        )

    for k in range(1, nlat):
        lat_copy(k).start()
    for k in range(1, nlat):
        lat_copy(k).wait()
    total = lar[0]
    for k in range(1, nlat):
        total = total + lar[k]
    ags[...] = total.astype(BF16)
    ag_o[lon] = total.astype(BF16)

    def gather_copy(k):
        peer = lon_peer(k)
        return pltpu.make_async_remote_copy(
            src_ref=ags,
            dst_ref=ag_o.at[lon],
            send_sem=q_send.at[k],
            recv_sem=q_recv.at[k],
            device_id=(lat, peer),
            device_id_type=MESH,
        )

    def start_gather(k, c):
        gather_copy(k).start()
        return c

    lax.fori_loop(1, nlon, start_gather, 0)

    def wait_tile(k, c):
        tile_copy(k).wait()
        return c

    lax.fori_loop(1, nlon, wait_tile, 0)
    for r in range(CAP):
        cn_o[r] = recv[work_tab[r]].astype(F32)
    for copy in edges:
        copy.wait()

    def wait_gather(k, c):
        gather_copy(k).wait()
        return c

    lax.fori_loop(1, nlon, wait_gather, 0)


def finish_kernel(
    nlat, nlon, scaling, hid, cg, cn, hg, ge, ag, hid_o, cn_o, hg_o, cg_o, wg_o, bg_o
):
    lat = lax.axis_index("lat")
    hid_o[...] = hid[...]
    cg_o[...] = cg[...]
    cn_o[...] = cn[...]
    lane64 = lane_iota(HID)
    keep_up = jnp.where(lat > 0, 1.0, 0.0).astype(F32)
    keep_down = jnp.where(lat < nlat - 1, 1.0, 0.0).astype(F32)
    left = ge[2].astype(F32)
    right = ge[3].astype(F32)
    for i in range(ROWS):
        row = hg[i]
        add_l = pltpu.roll(left, (LANES - 1 - i) % LANES, 1)
        add_r = pltpu.roll(right, LANES - 2 - i, 1)
        if i == 0:
            row = row + keep_up * ge[0].astype(F32)
            add_l = add_l + keep_up * pltpu.roll(ge[4].astype(F32), LANES - 17, 1)
            add_r = add_r + keep_up * pltpu.roll(ge[5].astype(F32), LANES - 18, 1)
        if i == ROWS - 1:
            row = row + keep_down * ge[1].astype(F32)
            add_l = add_l + keep_down * ge[6].astype(F32)
            add_r = add_r + keep_down * pltpu.roll(ge[7].astype(F32), LANES - 1, 1)
        row = row + jnp.where(lane64 == 0, add_l, jnp.where(lane64 == LANES - 1, add_r, 0.0))
        hg_o[pl.ds(i, HID, stride=ROWS), :] = row
    per = GATES // nlon
    bias = []
    for k in range(nlon):
        x = ag[k].astype(F32) * scaling
        whole = jnp.concatenate([x[:per], x[per:]], 1)
        wg_o[k * per : (k + 1) * per, :] = jnp.concatenate(
            [whole[:, d * GATES : d * GATES + TAP3] for d in range(3)], 1
        )
        bias.append(whole[:, LANES:GATES])
    bg_o[...] = jnp.concatenate(bias, 0).T[TAP3 - LANES : TAP3 - LANES + 1, :]


def body(forcing, hidden, cell, grad_hidden, grad_cell, wet_mask, tile_owner, w_gates, b_gates):
    nlat = lax.axis_size("lat")
    nlon = lax.axis_size("lon")
    per = GATES // nlon
    vmem = pl.BlockSpec(memory_space=pltpu.VMEM)
    smem = pl.BlockSpec(memory_space=pltpu.SMEM)
    cells = HID * ROWS
    sems = pltpu.SemaphoreType.DMA
    hid, cg, cn, hg, ge, ag = pl.pallas_call(
        functools.partial(step_kernel, nlat, nlon),
        out_shape=(
            jax.ShapeDtypeStruct((HID, ROWS, LANES), BF16),
            jax.ShapeDtypeStruct((cells, LANES), F32),
            jax.ShapeDtypeStruct((CAP, HID, 256), F32),
            jax.ShapeDtypeStruct((ROWS, HID, LANES), F32),
            jax.ShapeDtypeStruct((8, HID, LANES), BF16),
            jax.ShapeDtypeStruct((nlon, 2 * per, HALF), BF16),
        ),
        in_specs=[vmem] * 5 + [smem] * 2 + [vmem] * 2,
        out_specs=[vmem] * 6,
        scratch_shapes=[
            pltpu.VMEM((INP * ROWS, LANES), F32),
            pltpu.VMEM((cells, LANES), F32),
            pltpu.VMEM((cells, LANES), F32),
            pltpu.VMEM((cells, LANES), F32),
            pltpu.VMEM((cells, LANES), F32),
            pltpu.VMEM((cells, LANES), F32),
            pltpu.VMEM((GATES, 18 * LANES), BF16),
            pltpu.VMEM((3, GATES, GATES), BF16),
            pltpu.VMEM((3, GATES, GATES), BF16),
            pltpu.VMEM((GATES, LANES), F32),
            pltpu.VMEM((GATES, 20 * LANES), BF16),
            pltpu.VMEM((ROWS, HID, LANES), F32),
            pltpu.VMEM((TILES, HID, 256), BF16),
            pltpu.VMEM((nlon, HID, 256), BF16),
            pltpu.VMEM((nlon, HID, 256), BF16),
            pltpu.VMEM((GATES, 2 * HALF), F32),
            pltpu.VMEM((nlon, 2 * per, HALF), BF16),
            pltpu.VMEM((nlon, 2 * per, HALF), BF16),
            pltpu.VMEM((2 * per, HALF), F32),
            pltpu.VMEM((nlat, 2 * per, HALF), F32),
            pltpu.VMEM((2 * per, HALF), BF16),
            pltpu.VMEM((4, CH, LANES), BF16),
            pltpu.VMEM((8, CH, LANES), BF16),
            pltpu.VMEM((4, HID, LANES), BF16),
            sems((8,)),
            sems((8,)),
            sems((8,)),
            sems((8,)),
            sems((nlon,)),
            sems((nlon,)),
            sems((nlon,)),
            sems((nlon,)),
            sems((nlat,)),
            sems((nlat,)),
            sems((nlon,)),
            sems((nlon,)),
            pltpu.SMEM((nlon,), jnp.int32),
            pltpu.SMEM((CAP,), jnp.int32),
        ],
        compiler_params=pltpu.CompilerParams(
            collective_id=0, has_side_effects=True, vmem_limit_bytes=48 << 20
        ),
        name="step",
    )(
        forcing,
        hidden,
        cell,
        grad_hidden,
        grad_cell,
        wet_mask,
        tile_owner,
        w_gates,
        b_gates.reshape(1, GATES),
    )
    scaling = 1.0 / math.sqrt(float(nlat * nlon * CAP * 256))
    hid, cn, hg, cg, wg, bg = pl.pallas_call(
        functools.partial(finish_kernel, nlat, nlon, scaling),
        out_shape=(
            jax.ShapeDtypeStruct((HID, ROWS, LANES), BF16),
            jax.ShapeDtypeStruct((CAP, HID, 256), F32),
            jax.ShapeDtypeStruct((cells, LANES), F32),
            jax.ShapeDtypeStruct((cells, LANES), F32),
            jax.ShapeDtypeStruct((GATES, 3 * TAP3), F32),
            jax.ShapeDtypeStruct((1, GATES), F32),
        ),
        in_specs=[vmem] * 6,
        out_specs=[vmem] * 6,
        name="finish",
    )(hid, cg, cn, hg, ge, ag)
    return (
        hid,
        cn,
        hg.reshape(HID, ROWS, LANES),
        cg.reshape(HID, ROWS, LANES),
        wg,
        bg.reshape(GATES),
    )


def solution(mesh):
    return jax.shard_map(
        body,
        mesh=mesh,
        in_specs=(
            P(None, "lat", "lon"),
            P(None, "lat", "lon"),
            P(None, "lat", "lon"),
            P(None, "lat", "lon"),
            P(None, "lat", "lon"),
            P("lat", None),
            P("lat", None),
            P(),
            P(),
        ),
        out_specs=(
            P(None, "lat", "lon"),
            P(("lat", "lon"), None, None),
            P(None, "lat", "lon"),
            P(None, "lat", "lon"),
            P(),
            P(),
        ),
        check_vma=False,
    )
```

```python
import functools
import math

import jax
import jax.numpy as jnp
from jax import lax
from jax.experimental import pallas as pl
from jax.experimental.pallas import tpu as pltpu
from jax.sharding import PartitionSpec as P

MESH = pl.DeviceIdType.MESH
F32 = jnp.float32
BF16 = jnp.bfloat16
ROWS = 16
LANES = 128
INP = 16
HID = 64
CH = 80
GATES = 256
TAP3 = 240
CAP = 4
TILES = 8
PADK = 768


BATCHES = (0, 7, 10, 19, 26, 31)


def lane_iota(rows):
    return lax.broadcasted_iota(jnp.int32, (rows, LANES), 1)


def row_of(i):
    return pl.ds(pl.multiple_of(i * LANES, LANES), LANES)


def sigmoid(x):
    return 0.5 * jnp.tanh(0.5 * x) + 0.5


def step_kernel(
    nlat,
    nlon,
    forcing_hbm,
    hidden_hbm,
    cell_hbm,
    grad_h_hbm,
    grad_c_hbm,
    wet,
    owner,
    w_hbm,
    b_ref,
    hid_o,
    cg_o,
    cn_o,
    hg_o,
    ge_o,
    ag_o,
    forcing,
    hidden,
    cell,
    grad_h,
    grad_c,
    w_ref,
    f32f,
    f32h,
    f32c,
    f32gh,
    f32gc,
    hid32,
    e,
    wp,
    bcol,
    delta,
    crow,
    tiles,
    slots,
    recv,
    halves,
    pair_half,
    wgs,
    rsr,
    las,
    lar,
    ags,
    hs,
    hr,
    gs,
    in_sem,
    h_send,
    h_recv,
    g_send,
    g_recv,
    a_send,
    a_recv,
    c_send,
    c_recv,
    r_send,
    r_recv,
    l_send,
    l_recv,
    q_send,
    q_recv,
    slot_tab,
):
    lat = lax.axis_index("lat")
    lon = lax.axis_index("lon")
    up = lax.rem(lat + nlat - 1, nlat)
    down = lax.rem(lat + 1, nlat)
    left = lax.rem(lon + nlon - 1, nlon)
    right = lax.rem(lon + 1, nlon)

    def lon_peer(k):
        return lax.rem(lon + k, nlon)

    def lat_peer(k):
        return lax.rem(lat + k, nlat)

    core = lax.rem(lat, 2)
    partner = lat + 1 - 2 * core
    places = nlat // 2

    def drain(ref, sem):
        pltpu.make_async_copy(ref, ref, sem).wait()

    loads = [
        pltpu.make_async_copy(src, dst, in_sem.at[k])
        for k, (src, dst) in enumerate(
            (
                (forcing_hbm, forcing),
                (hidden_hbm, hidden),
                (cell_hbm, cell),
                (grad_h_hbm, grad_h),
                (grad_c_hbm, grad_c),
                (w_hbm, w_ref),
            )
        )
    ]
    for load in loads:
        load.start()

    diagonals = ((up, left), (up, right), (down, left), (down, right))

    barrier = pltpu.get_barrier_semaphore()
    for place in diagonals:
        pl.semaphore_signal(barrier, inc=1, device_id=place, device_id_type=MESH)

    def greet_lat(k, c):
        pl.semaphore_signal(barrier, inc=1, device_id=(lat_peer(k), lon), device_id_type=MESH)
        return c

    lax.fori_loop(1, nlat, greet_lat, 0)

    def greet_lon(k, c):
        pl.semaphore_signal(barrier, inc=1, device_id=(lat, lon_peer(k)), device_id_type=MESH)
        return c

    lax.fori_loop(1, nlon, greet_lon, 0)

    loads[0].wait()
    loads[1].wait()
    f32f[...] = forcing[...].astype(F32).reshape(INP * ROWS, LANES)
    f32h[...] = hidden[...].astype(F32).reshape(HID * ROWS, LANES)
    lane80 = lane_iota(CH)

    def field_row(i):
        return jnp.concatenate(
            [f32f[pl.ds(i, INP, stride=ROWS), :], f32h[pl.ds(i, HID, stride=ROWS), :]], 0
        )

    edge_l = jnp.zeros((CH, LANES), F32)
    edge_r = jnp.zeros((CH, LANES), F32)
    for i in range(ROWS):
        row = field_row(i)
        e[CH : 2 * CH, (i + 1) * LANES : (i + 2) * LANES] = row.astype(BF16)
        e[0:CH, (i + 1) * LANES : (i + 2) * LANES] = pltpu.roll(row, 1, 1).astype(BF16)
        e[2 * CH : TAP3, (i + 1) * LANES : (i + 2) * LANES] = pltpu.roll(
            row, LANES - 1, 1
        ).astype(BF16)
        edge_l = jnp.where(lane80 == i, row[:, 0:1], edge_l)
        edge_r = jnp.where(lane80 == i, row[:, LANES - 1 : LANES], edge_r)
        if i == 0:
            hs[0] = row.astype(BF16)
        if i == ROWS - 1:
            hs[1] = row.astype(BF16)
    hs[2] = edge_l.astype(BF16)
    hs[3] = edge_r.astype(BF16)

    pl.semaphore_wait(barrier, nlon - 1 + nlat - 1 + 4)

    halo_plan = (
        (1, 0, (down, lon)),
        (0, 1, (up, lon)),
        (3, 2, (lat, right)),
        (2, 3, (lat, left)),
        (1, 4, (down, right)),
        (1, 5, (down, left)),
        (0, 6, (up, right)),
        (0, 7, (up, left)),
    )
    halo = []
    for src, dst, place in halo_plan:
        copy = pltpu.make_async_remote_copy(
            src_ref=hs.at[src],
            dst_ref=hr.at[dst],
            send_sem=h_send.at[dst],
            recv_sem=h_recv.at[dst],
            device_id=place,
            device_id_type=MESH,
        )
        copy.start()
        halo.append(copy)

    for load in loads[2:]:
        load.wait()
    f32c[...] = cell[...].astype(F32).reshape(HID * ROWS, LANES)
    f32gh[...] = grad_h[...].astype(F32).reshape(HID * ROWS, LANES)
    f32gc[...] = grad_c[...].astype(F32).reshape(HID * ROWS, LANES)
    for dr in range(3):
        part = jnp.concatenate(
            [
                w_ref[dr * TAP3 : (dr + 1) * TAP3, :].astype(F32),
                jnp.zeros((GATES - TAP3, GATES), F32),
            ],
            0,
        )
        wp[dr] = part.T.astype(BF16)
    bcol[...] = jnp.broadcast_to(b_ref[...], (LANES, GATES)).T
    ones_row = lax.broadcasted_iota(jnp.int32, (GATES - TAP3, 18 * LANES), 0) == 0
    e[TAP3:GATES, :] = jnp.where(ones_row, 1.0, 0.0).astype(BF16)
    delta[:, 0 : 2 * LANES] = jnp.zeros((GATES, 2 * LANES), BF16)
    delta[:, 18 * LANES : 20 * LANES] = jnp.zeros((GATES, 2 * LANES), BF16)

    base = lon * TILES
    wet_here = [wet[0, base + q] for q in range(TILES)]
    own_here = [owner[0, base + q] for q in range(TILES)]

    def plan_slot(o, c):
        source = jnp.int32(0)
        for q in range(TILES):
            source = source + jnp.where((wet_here[q] > 0) & (own_here[q] == o), q, 0)
        slot_tab[o] = source
        return c

    lax.fori_loop(0, nlon, plan_slot, 0)

    lane64 = lane_iota(HID)
    live = jnp.zeros((HID, LANES), F32)
    for q in range(TILES):
        live = jnp.where(
            lane64 // 16 == q, jnp.where(wet_here[q] > 0, 1.0, 0.0).astype(F32), live
        )

    for copy in halo:
        copy.wait()

    keep_up = jnp.where(lat > 0, 1.0, 0.0).astype(F32)
    keep_down = jnp.where(lat < nlat - 1, 1.0, 0.0).astype(F32)
    from_left = hr[2].astype(F32)
    from_right = hr[3].astype(F32)
    for i in range(ROWS):
        cols = slice((i + 1) * LANES, (i + 2) * LANES)
        a = e[0:CH, cols].astype(F32)
        e[0:CH, cols] = jnp.where(
            lane80 == 0, pltpu.roll(from_left, (LANES - i) % LANES, 1), a
        ).astype(BF16)
        a = e[2 * CH : TAP3, cols].astype(F32)
        e[2 * CH : TAP3, cols] = jnp.where(
            lane80 == LANES - 1, pltpu.roll(from_right, LANES - 1 - i, 1), a
        ).astype(BF16)
    for block, keep, mid, lft, rgt in ((0, keep_up, 0, 4, 5), (17, keep_down, 1, 6, 7)):
        cols = slice(block * LANES, (block + 1) * LANES)
        row = hr[mid].astype(F32)
        e[CH : 2 * CH, cols] = (row * keep).astype(BF16)
        a = jnp.where(
            lane80 == 0, pltpu.roll(hr[lft].astype(F32), 1, 1), pltpu.roll(row, 1, 1)
        )
        e[0:CH, cols] = (a * keep).astype(BF16)
        a = jnp.where(
            lane80 == LANES - 1,
            pltpu.roll(hr[rgt].astype(F32), LANES - 1, 1),
            pltpu.roll(row, LANES - 1, 1),
        )
        e[2 * CH : TAP3, cols] = (a * keep).astype(BF16)

    def forward(c, carry):
        pre = jnp.zeros((GATES, 2 * LANES), F32)
        for dr in range(3):
            cols = pl.ds(pl.multiple_of(c * 2 * LANES + dr * LANES, LANES), 2 * LANES)
            pre = pre + jnp.dot(wp[dr], e[:, cols], preferred_element_type=F32)
        for s in range(2):
            i = c * 2 + s
            full = pre[:, s * LANES : (s + 1) * LANES] + bcol[...]
            g_in = sigmoid(full[0:HID])
            g_forget = sigmoid(full[HID : 2 * HID])
            g_out = sigmoid(full[2 * HID : 3 * HID])
            cand = jnp.tanh(full[3 * HID :])
            old = f32c[pl.ds(i, HID, stride=ROWS), :]
            new = g_forget * old + g_in * cand
            squash = jnp.tanh(new)
            crow[i] = new
            hid32[pl.ds(i, HID, stride=ROWS), :] = live * g_out * squash
            back_h = live * f32gh[pl.ds(i, HID, stride=ROWS), :]
            back_c = live * f32gc[pl.ds(i, HID, stride=ROWS), :] + back_h * g_out * (
                1.0 - squash * squash
            )
            cell_back = back_c * g_forget
            cg_o[pl.ds(i, HID, stride=ROWS), :] = cell_back
            back_in = back_c * g_in
            cols = row_of(i + 2)
            delta[0:HID, cols] = (back_in * cand * (1.0 - g_in)).astype(BF16)
            delta[HID : 2 * HID, cols] = (cell_back * old * (1.0 - g_forget)).astype(BF16)
            delta[2 * HID : 3 * HID, cols] = (
                back_h * squash * g_out * (1.0 - g_out)
            ).astype(BF16)
            delta[3 * HID :, cols] = (back_in * (1.0 - cand * cand)).astype(BF16)
        return carry

    lax.fori_loop(0, ROWS // 2, forward, 0)

    lane16 = lane_iota(16) // 16

    def regroup(step, carry):
        half = step // 4
        subs = pl.ds(pl.multiple_of(lax.rem(step, 4) * 16, 16), 16)
        x = [crow[half * 8 + k, subs, :] for k in range(8)]
        for s in (1, 2, 4):
            low = (lane16 // s) % 2 == 0
            y = list(x)
            for k in range(8):
                if (k // s) % 2 == 0:
                    a, b = x[k], x[k + s]
                    y[k] = jnp.where(low, a, pltpu.roll(b, 16 * s, 1))
                    y[k + s] = jnp.where(low, pltpu.roll(a, LANES - 16 * s, 1), b)
            x = y
        for q in range(8):
            tiles[q, subs, row_of(half)] = x[q].astype(BF16)
        return carry

    lax.fori_loop(0, 8, regroup, 0)

    def fill(o, carry):
        slots[o] = tiles[slot_tab[o]]
        return carry

    lax.fori_loop(0, nlon, fill, 0)
    recv[lon] = slots[lon]

    def tile_copy(k):
        peer = lon_peer(k)
        return pltpu.make_async_remote_copy(
            src_ref=slots.at[peer],
            dst_ref=recv.at[lon],
            send_sem=a_send,
            recv_sem=a_recv,
            device_id=(lat, peer),
            device_id_type=MESH,
        )

    def start_tiles(first, last):
        def start(k, c):
            tile_copy(k).start()
            return c

        lax.fori_loop(first, last, start, 0)

    cuts = [1 + (nlon - 1) * n // 31 for n in BATCHES]
    start_tiles(cuts[0], cuts[1])

    for dr in range(3):
        rows = TAP3 if dr < 2 else GATES
        terms = lax.dot_general(
            e[0:rows, dr * LANES : (dr + ROWS) * LANES],
            delta[:, 2 * LANES : 18 * LANES],
            (((1,), (1,)), ((), ())),
            preferred_element_type=F32,
        )
        for half in range(2):
            halves[half, dr * TAP3 : dr * TAP3 + rows, :] = terms[
                :, half * LANES : (half + 1) * LANES
            ]
    filler = 2 * TAP3 + GATES
    halves[:, filler:PADK, :] = jnp.zeros((2, PADK - filler, LANES), F32)
    pair = pltpu.make_async_remote_copy(
        src_ref=halves.at[1 - core],
        dst_ref=pair_half,
        send_sem=c_send.at[0],
        recv_sem=c_recv.at[0],
        device_id=(partner, lon),
        device_id_type=MESH,
    )
    pair.start()
    start_tiles(cuts[1], cuts[2])

    colv_l = jnp.zeros((HID, LANES), F32)
    colv_r = jnp.zeros((HID, LANES), F32)
    for c in range(9):
        acc = jnp.zeros((TAP3, 2 * LANES), F32)
        for dr in range(3):
            start = (2 * c + 2 - dr) * LANES
            acc = acc + jnp.dot(
                w_ref[dr * TAP3 : (dr + 1) * TAP3, :],
                delta[:, start : start + 2 * LANES],
                preferred_element_type=F32,
            )
        for s in range(2):
            r = 2 * c + s
            part = acc[:, s * LANES : (s + 1) * LANES]
            s0 = part[INP:CH]
            s1 = part[CH + INP : 2 * CH]
            s2 = part[2 * CH + INP : TAP3]
            colv_l = jnp.where(lane64 == r, s0[:, 0:1], colv_l)
            colv_r = jnp.where(lane64 == r, s2[:, LANES - 1 : LANES], colv_r)
            total = (
                s1
                + jnp.where(lane64 < LANES - 1, pltpu.roll(s0, LANES - 1, 1), 0.0)
                + jnp.where(lane64 > 0, pltpu.roll(s2, 1, 1), 0.0)
            )
            if r == 0:
                gs[0] = total.astype(BF16)
            elif r == 17:
                gs[1] = total.astype(BF16)
            else:
                hg_o[r - 1] = total
    gs[2] = colv_l.astype(BF16)
    gs[3] = colv_r.astype(BF16)
    grad_plan = (
        (1, 0, (down, lon)),
        (0, 1, (up, lon)),
        (3, 2, (lat, right)),
        (2, 3, (lat, left)),
        (3, 4, (down, right)),
        (2, 5, (down, left)),
        (3, 6, (up, right)),
        (2, 7, (up, left)),
    )
    edges = []
    for src, dst, place in grad_plan:
        copy = pltpu.make_async_remote_copy(
            src_ref=gs.at[src],
            dst_ref=ge_o.at[dst],
            send_sem=g_send.at[dst],
            recv_sem=g_recv.at[dst],
            device_id=place,
            device_id_type=MESH,
        )
        copy.start()
        edges.append(copy)
    per = PADK // nlon
    pair.wait()

    def pack_terms(k, carry):
        rows = pl.ds(pl.multiple_of(k * per, per), per)
        wgs[k] = (halves[core, rows, :] + pair_half[rows, :]).astype(BF16)
        return carry

    lax.fori_loop(0, nlon, pack_terms, 0, unroll=4)
    rsr[lon] = wgs[lon]

    def start_scatter(k, c):
        peer = lon_peer(k)
        pltpu.make_async_remote_copy(
            src_ref=wgs.at[peer],
            dst_ref=rsr.at[lon],
            send_sem=r_send,
            recv_sem=r_recv,
            device_id=(lat, peer),
            device_id_type=MESH,
        ).start()
        return c

    lax.fori_loop(1, nlon, start_scatter, 0)
    start_tiles(cuts[2], cuts[3])
    hid_o[...] = hid32[...].reshape(HID, ROWS, LANES).astype(BF16)

    def plan_work(d, carry):
        count, work = carry
        has = jnp.int32(0)
        for q in range(TILES):
            has = has + jnp.where(
                (wet[0, d * TILES + q] > 0) & (owner[0, d * TILES + q] == lon), 1, 0
            )
        work = tuple(
            work[r] + jnp.where((has > 0) & (count == r), d, 0) for r in range(CAP)
        )
        return (count + has, work)

    _, work = lax.fori_loop(
        0, nlon, plan_work, (jnp.int32(0), tuple(jnp.int32(0) for _ in range(CAP)))
    )

    drain(rsr.at[pl.ds(0, nlon - 1)], r_recv)
    lon_sum = lax.fori_loop(
        0, nlon, lambda k, t: t + rsr[k].astype(F32), jnp.zeros((per, LANES), F32), unroll=4
    )
    las[...] = lon_sum
    lar[lat // 2] = lon_sum
    across = []
    for k in range(1, places):
        copy = pltpu.make_async_remote_copy(
            src_ref=las,
            dst_ref=lar.at[lat // 2],
            send_sem=l_send.at[k],
            recv_sem=l_recv.at[k],
            device_id=(lat_peer(2 * k), lon),
            device_id_type=MESH,
        )
        copy.start()
        across.append(copy)
    start_tiles(cuts[3], cuts[4])
    for copy in across:
        copy.wait()
    total = lar[0]
    for k in range(1, places):
        total = total + lar[k]
    ags[...] = total.astype(BF16)
    ag_o[core, lon] = total.astype(BF16)

    def start_gather(k, c):
        pltpu.make_async_remote_copy(
            src_ref=ags,
            dst_ref=ag_o.at[core, lon],
            send_sem=q_send,
            recv_sem=q_recv,
            device_id=(lat, lon_peer(k)),
            device_id_type=MESH,
        ).start()
        return c

    lax.fori_loop(1, nlon, start_gather, 0)
    start_tiles(cuts[4], cuts[5])
    for copy in edges:
        copy.wait()
    drain(ag_o.at[core, pl.ds(0, nlon - 1)], q_recv)
    last = pltpu.make_async_remote_copy(
        src_ref=ag_o.at[core],
        dst_ref=ag_o.at[core],
        send_sem=c_send.at[1],
        recv_sem=c_recv.at[1],
        device_id=(partner, lon),
        device_id_type=MESH,
    )
    last.start()
    drain(recv.at[pl.ds(0, nlon - 1)], a_recv)
    for r in range(CAP):
        cn_o[r] = recv[work[r]].astype(F32)
    drain(rsr.at[pl.ds(0, nlon - 1)], r_send)
    drain(ag_o.at[core, pl.ds(0, nlon - 1)], q_send)
    drain(recv.at[pl.ds(0, nlon - 1)], a_send)
    last.wait()


def finish_kernel(
    nlat, nlon, scaling, hid, cg, cn, hg, ge, ag, hid_o, cn_o, hg_o, cg_o, wg_o, bg_o
):
    lat = lax.axis_index("lat")
    hid_o[...] = hid[...]
    cg_o[...] = cg[...]
    cn_o[...] = cn[...]
    lane64 = lane_iota(HID)
    keep_up = jnp.where(lat > 0, 1.0, 0.0).astype(F32)
    keep_down = jnp.where(lat < nlat - 1, 1.0, 0.0).astype(F32)
    left = ge[2].astype(F32)
    right = ge[3].astype(F32)
    for i in range(ROWS):
        row = hg[i]
        add_l = pltpu.roll(left, (LANES - 1 - i) % LANES, 1)
        add_r = pltpu.roll(right, LANES - 2 - i, 1)
        if i == 0:
            row = row + keep_up * ge[0].astype(F32)
            add_l = add_l + keep_up * pltpu.roll(ge[4].astype(F32), LANES - 17, 1)
            add_r = add_r + keep_up * pltpu.roll(ge[5].astype(F32), LANES - 18, 1)
        if i == ROWS - 1:
            row = row + keep_down * ge[1].astype(F32)
            add_l = add_l + keep_down * ge[6].astype(F32)
            add_r = add_r + keep_down * pltpu.roll(ge[7].astype(F32), LANES - 1, 1)
        row = row + jnp.where(lane64 == 0, add_l, jnp.where(lane64 == LANES - 1, add_r, 0.0))
        hg_o[pl.ds(i, HID, stride=ROWS), :] = row
    low = ag[0].astype(F32).reshape(PADK, LANES) * scaling
    high = ag[1].astype(F32).reshape(PADK, LANES) * scaling
    wg_o[:, :LANES] = low[: 3 * TAP3]
    wg_o[:, LANES:] = high[: 3 * TAP3]
    bg_o[:, :LANES] = low[3 * TAP3 : 3 * TAP3 + 1]
    bg_o[:, LANES:] = high[3 * TAP3 : 3 * TAP3 + 1]


def body(forcing, hidden, cell, grad_hidden, grad_cell, wet_mask, tile_owner, w_gates, b_gates):
    nlat = lax.axis_size("lat")
    nlon = lax.axis_size("lon")
    per = PADK // nlon
    anyw = pl.BlockSpec(memory_space=pltpu.HBM)
    vmem = pl.BlockSpec(memory_space=pltpu.VMEM)
    smem = pl.BlockSpec(memory_space=pltpu.SMEM)
    cells = HID * ROWS

    def in_hbm(x):
        return pltpu.with_memory_space_constraint(x, pltpu.HBM)

    sems = pltpu.SemaphoreType.DMA
    hid, cg, cn, hg, ge, ag = pl.pallas_call(
        functools.partial(step_kernel, nlat, nlon),
        out_shape=(
            jax.ShapeDtypeStruct((HID, ROWS, LANES), BF16),
            jax.ShapeDtypeStruct((cells, LANES), F32),
            jax.ShapeDtypeStruct((CAP, HID, 256), F32),
            jax.ShapeDtypeStruct((ROWS, HID, LANES), F32),
            jax.ShapeDtypeStruct((8, HID, LANES), BF16),
            jax.ShapeDtypeStruct((2, nlon, per, LANES), BF16),
        ),
        in_specs=[anyw] * 5 + [smem] * 2 + [anyw, vmem],
        out_specs=[vmem] * 6,
        scratch_shapes=[
            pltpu.VMEM((INP, ROWS, LANES), BF16),
            pltpu.VMEM((HID, ROWS, LANES), BF16),
            pltpu.VMEM((HID, ROWS, LANES), BF16),
            pltpu.VMEM((HID, ROWS, LANES), BF16),
            pltpu.VMEM((HID, ROWS, LANES), BF16),
            pltpu.VMEM((3 * TAP3, GATES), BF16),
            pltpu.VMEM((INP * ROWS, LANES), F32),
            pltpu.VMEM((cells, LANES), F32),
            pltpu.VMEM((cells, LANES), F32),
            pltpu.VMEM((cells, LANES), F32),
            pltpu.VMEM((cells, LANES), F32),
            pltpu.VMEM((cells, LANES), F32),
            pltpu.VMEM((GATES, 18 * LANES), BF16),
            pltpu.VMEM((3, GATES, GATES), BF16),
            pltpu.VMEM((GATES, LANES), F32),
            pltpu.VMEM((GATES, 20 * LANES), BF16),
            pltpu.VMEM((ROWS, HID, LANES), F32),
            pltpu.VMEM((TILES, HID, 256), BF16),
            pltpu.VMEM((nlon, HID, 256), BF16),
            pltpu.VMEM((nlon, HID, 256), BF16),
            pltpu.VMEM((2, PADK, LANES), F32),
            pltpu.VMEM((PADK, LANES), F32),
            pltpu.VMEM((nlon, per, LANES), BF16),
            pltpu.VMEM((nlon, per, LANES), BF16),
            pltpu.VMEM((per, LANES), F32),
            pltpu.VMEM((nlat // 2, per, LANES), F32),
            pltpu.VMEM((per, LANES), BF16),
            pltpu.VMEM((4, CH, LANES), BF16),
            pltpu.VMEM((8, CH, LANES), BF16),
            pltpu.VMEM((4, HID, LANES), BF16),
            sems((6,)),
            sems((8,)),
            sems((8,)),
            sems((8,)),
            sems((8,)),
            sems,
            sems,
            sems((2,)),
            sems((2,)),
            sems,
            sems,
            sems((nlat // 2,)),
            sems((nlat // 2,)),
            sems,
            sems,
            pltpu.SMEM((nlon,), jnp.int32),
        ],
        compiler_params=pltpu.CompilerParams(
            collective_id=0, has_side_effects=True, vmem_limit_bytes=40 << 20
        ),
        name="step",
    )(
        in_hbm(forcing),
        in_hbm(hidden),
        in_hbm(cell),
        in_hbm(grad_hidden),
        in_hbm(grad_cell),
        wet_mask,
        tile_owner,
        in_hbm(w_gates.T),
        b_gates.reshape(1, GATES),
    )
    scaling = 1.0 / math.sqrt(float(nlat * nlon * CAP * 256))
    hid, cn, hg, cg, wg, bg = pl.pallas_call(
        functools.partial(finish_kernel, nlat, nlon, scaling),
        out_shape=(
            jax.ShapeDtypeStruct((HID, ROWS, LANES), BF16),
            jax.ShapeDtypeStruct((CAP, HID, 256), F32),
            jax.ShapeDtypeStruct((cells, LANES), F32),
            jax.ShapeDtypeStruct((cells, LANES), F32),
            jax.ShapeDtypeStruct((3 * TAP3, GATES), F32),
            jax.ShapeDtypeStruct((1, GATES), F32),
        ),
        in_specs=[vmem] * 6,
        out_specs=[vmem] * 6,
        compiler_params=pltpu.CompilerParams(vmem_limit_bytes=12 << 20),
        name="finish",
    )(hid, cg, cn, hg, ge, ag)
    return (
        hid,
        cn,
        hg.reshape(HID, ROWS, LANES),
        cg.reshape(HID, ROWS, LANES),
        wg.T,
        bg.reshape(GATES),
    )


def solution(mesh):
    return jax.shard_map(
        body,
        mesh=mesh,
        in_specs=(
            P(None, "lat", "lon"),
            P(None, "lat", "lon"),
            P(None, "lat", "lon"),
            P(None, "lat", "lon"),
            P(None, "lat", "lon"),
            P("lat", None),
            P("lat", None),
            P(),
            P(),
        ),
        out_specs=(
            P(None, "lat", "lon"),
            P(("lat", "lon"), None, None),
            P(None, "lat", "lon"),
            P(None, "lat", "lon"),
            P(),
            P(),
        ),
        check_vma=False,
    )
```

```python
import functools
import math

import jax
import jax.numpy as jnp
from jax import lax
from jax.experimental import pallas as pl
from jax.experimental.pallas import tpu as pltpu
from jax.sharding import PartitionSpec as P

MESH = pl.DeviceIdType.MESH
F32 = jnp.float32
BF16 = jnp.bfloat16
ROWS = 16
LANES = 128
INP = 16
HID = 64
CH = 80
GATES = 256
TAP3 = 240
CAP = 4
TILES = 8
PADK = 768


BATCHES = (0, 0, 11, 25, 31)
UNROLL = 1


def far_first(nx):
    steps = [(dx, dz, dy) for dx in range(nx) for dz in range(2) for dy in range(4)]
    steps.sort(key=lambda t: -(min(t[0], nx - t[0]) + t[1] + min(t[2], 4 - t[2])))
    return steps[:-1]


def lane_iota(rows):
    return lax.broadcasted_iota(jnp.int32, (rows, LANES), 1)


def row_of(i):
    return pl.ds(pl.multiple_of(i * LANES, LANES), LANES)


def sigmoid(x):
    return 0.5 * jnp.tanh(0.5 * x) + 0.5


def step_kernel(
    nlat,
    nlon,
    forcing_hbm,
    hidden_hbm,
    cell_hbm,
    grad_h_hbm,
    grad_c_hbm,
    wet_hbm,
    owner_hbm,
    w_hbm,
    b_hbm,
    hid_o,
    cg_o,
    cn_o,
    hg_o,
    ge_o,
    ag_o,
    forcing,
    hidden,
    cell,
    grad_h,
    grad_c,
    w_ref,
    b_ref,
    wet,
    owner,
    f32f,
    f32h,
    f32c,
    f32gh,
    f32gc,
    hid32,
    e,
    wp,
    bcol,
    delta,
    crow,
    tiles,
    slots,
    recv,
    halves,
    pair_half,
    wgs,
    rsr,
    las,
    lar,
    ags,
    hs,
    hr,
    gs,
    in_sem,
    h_send,
    h_recv,
    g_send,
    g_recv,
    a_send,
    a_recv,
    c_send,
    c_recv,
    r_send,
    r_recv,
    l_send,
    l_recv,
    q_send,
    q_recv,
    slot_tab,
):
    lat = lax.axis_index("lat")
    lon = lax.axis_index("lon")
    up = lax.rem(lat + nlat - 1, nlat)
    down = lax.rem(lat + 1, nlat)
    left = lax.rem(lon + nlon - 1, nlon)
    right = lax.rem(lon + 1, nlon)

    def lon_peer(k):
        return lax.rem(lon + k, nlon)

    nx = nlon // 8
    at_x, at_z, at_y = lon // 8, lax.rem(lon // 4, 2), lax.rem(lon, 4)
    xs = [lax.rem(at_x + d, nx) * 8 for d in range(nx)]
    zs = [at_z * 4, (1 - at_z) * 4]
    ys = [lax.rem(at_y + d, 4) for d in range(4)]
    peers = [xs[dx] + zs[dz] + ys[dy] for dx, dz, dy in far_first(nx)]

    def lat_peer(k):
        return lax.rem(lat + k, nlat)

    core = lax.rem(lat, 2)
    partner = lat + 1 - 2 * core
    places = nlat // 2

    def drain(ref, sem):
        pltpu.make_async_copy(ref, ref, sem).wait()

    loads = [
        pltpu.make_async_copy(src, dst, in_sem.at[k])
        for k, (src, dst) in enumerate(
            (
                (forcing_hbm, forcing),
                (hidden_hbm, hidden),
                (cell_hbm, cell),
                (grad_h_hbm, grad_h),
                (grad_c_hbm, grad_c),
                (w_hbm, w_ref),
                (b_hbm, b_ref),
                (wet_hbm, wet),
                (owner_hbm, owner),
            )
        )
    ]
    for load in loads[:2]:
        load.start()

    diagonals = ((up, left), (up, right), (down, left), (down, right))

    barrier = pltpu.get_barrier_semaphore()
    for place in diagonals:
        pl.semaphore_signal(barrier, inc=1, device_id=place, device_id_type=MESH)

    for peer in peers:
        pl.semaphore_signal(barrier, inc=1, device_id=(lat, peer), device_id_type=MESH)
    for k in range(1, nlat):
        pl.semaphore_signal(barrier, inc=1, device_id=(lat_peer(k), lon), device_id_type=MESH)

    for load in loads[2:]:
        load.start()

    loads[0].wait()
    loads[1].wait()
    f32f[...] = forcing[...].astype(F32).reshape(INP * ROWS, LANES)
    f32h[...] = hidden[...].astype(F32).reshape(HID * ROWS, LANES)
    lane80 = lane_iota(CH)

    def field_row(i):
        return jnp.concatenate(
            [f32f[pl.ds(i, INP, stride=ROWS), :], f32h[pl.ds(i, HID, stride=ROWS), :]], 0
        )

    edge_l = jnp.zeros((CH, LANES), F32)
    edge_r = jnp.zeros((CH, LANES), F32)
    for i in range(ROWS):
        row = field_row(i)
        e[CH : 2 * CH, (i + 1) * LANES : (i + 2) * LANES] = row.astype(BF16)
        e[0:CH, (i + 1) * LANES : (i + 2) * LANES] = pltpu.roll(row, 1, 1).astype(BF16)
        e[2 * CH : TAP3, (i + 1) * LANES : (i + 2) * LANES] = pltpu.roll(
            row, LANES - 1, 1
        ).astype(BF16)
        edge_l = jnp.where(lane80 == i, row[:, 0:1], edge_l)
        edge_r = jnp.where(lane80 == i, row[:, LANES - 1 : LANES], edge_r)
        if i == 0:
            hs[0] = row.astype(BF16)
        if i == ROWS - 1:
            hs[1] = row.astype(BF16)
    hs[2] = edge_l.astype(BF16)
    hs[3] = edge_r.astype(BF16)

    pl.semaphore_wait(barrier, nlon - 1 + nlat - 1 + 4)

    halo_plan = (
        (1, 0, (down, lon)),
        (0, 1, (up, lon)),
        (3, 2, (lat, right)),
        (2, 3, (lat, left)),
        (1, 4, (down, right)),
        (1, 5, (down, left)),
        (0, 6, (up, right)),
        (0, 7, (up, left)),
    )
    halo = []
    for src, dst, place in halo_plan:
        copy = pltpu.make_async_remote_copy(
            src_ref=hs.at[src],
            dst_ref=hr.at[dst],
            send_sem=h_send.at[dst],
            recv_sem=h_recv.at[dst],
            device_id=place,
            device_id_type=MESH,
        )
        copy.start()
        halo.append(copy)

    for load in loads[2:]:
        load.wait()
    f32c[...] = cell[...].astype(F32).reshape(HID * ROWS, LANES)
    f32gh[...] = grad_h[...].astype(F32).reshape(HID * ROWS, LANES)
    f32gc[...] = grad_c[...].astype(F32).reshape(HID * ROWS, LANES)
    for dr in range(3):
        part = jnp.concatenate(
            [
                w_ref[dr * TAP3 : (dr + 1) * TAP3, :].astype(F32),
                jnp.zeros((GATES - TAP3, GATES), F32),
            ],
            0,
        )
        wp[dr] = part.T.astype(BF16)
    bcol[...] = jnp.broadcast_to(b_ref[...], (LANES, GATES)).T
    ones_row = lax.broadcasted_iota(jnp.int32, (GATES - TAP3, 18 * LANES), 0) == 0
    e[TAP3:GATES, :] = jnp.where(ones_row, 1.0, 0.0).astype(BF16)
    delta[:, 0 : 2 * LANES] = jnp.zeros((GATES, 2 * LANES), BF16)
    delta[:, 18 * LANES : 20 * LANES] = jnp.zeros((GATES, 2 * LANES), BF16)

    base = lon * TILES
    wet_here = [wet[0, base + q] for q in range(TILES)]
    own_here = [owner[0, base + q] for q in range(TILES)]

    def plan_slot(o, c):
        source = jnp.int32(0)
        for q in range(TILES):
            source = source + jnp.where((wet_here[q] > 0) & (own_here[q] == o), q, 0)
        slot_tab[o] = source
        return c

    lax.fori_loop(0, nlon, plan_slot, 0, unroll=4)

    lane64 = lane_iota(HID)
    live = jnp.zeros((HID, LANES), F32)
    for q in range(TILES):
        live = jnp.where(
            lane64 >> 4 == q, jnp.where(wet_here[q] > 0, 1.0, 0.0).astype(F32), live
        )

    for copy in halo[2:4]:
        copy.wait()

    keep_up = jnp.where(lat > 0, 1.0, 0.0).astype(F32)
    keep_down = jnp.where(lat < nlat - 1, 1.0, 0.0).astype(F32)
    from_left = hr[2].astype(F32)
    from_right = hr[3].astype(F32)
    for i in range(ROWS):
        cols = slice((i + 1) * LANES, (i + 2) * LANES)
        a = e[0:CH, cols].astype(F32)
        e[0:CH, cols] = jnp.where(
            lane80 == 0, pltpu.roll(from_left, (LANES - i) % LANES, 1), a
        ).astype(BF16)
        a = e[2 * CH : TAP3, cols].astype(F32)
        e[2 * CH : TAP3, cols] = jnp.where(
            lane80 == LANES - 1, pltpu.roll(from_right, LANES - 1 - i, 1), a
        ).astype(BF16)
    def forward(c, carry):
        pre = jnp.zeros((GATES, 2 * LANES), F32)
        for dr in range(3):
            cols = pl.ds(pl.multiple_of(c * 2 * LANES + dr * LANES, LANES), 2 * LANES)
            pre = pre + jnp.dot(wp[dr], e[:, cols], preferred_element_type=F32)
        for s in range(2):
            i = c * 2 + s
            full = pre[:, s * LANES : (s + 1) * LANES] + bcol[...]
            g_in = sigmoid(full[0:HID])
            g_forget = sigmoid(full[HID : 2 * HID])
            g_out = sigmoid(full[2 * HID : 3 * HID])
            cand = jnp.tanh(full[3 * HID :])
            old = f32c[pl.ds(i, HID, stride=ROWS), :]
            new = g_forget * old + g_in * cand
            squash = jnp.tanh(new)
            crow[i] = new
            hid32[pl.ds(i, HID, stride=ROWS), :] = live * g_out * squash
            back_h = live * f32gh[pl.ds(i, HID, stride=ROWS), :]
            back_c = live * f32gc[pl.ds(i, HID, stride=ROWS), :] + back_h * g_out * (
                1.0 - squash * squash
            )
            cell_back = back_c * g_forget
            cg_o[pl.ds(i, HID, stride=ROWS), :] = cell_back
            back_in = back_c * g_in
            cols = row_of(i + 2)
            delta[0:HID, cols] = (back_in * cand * (1.0 - g_in)).astype(BF16)
            delta[HID : 2 * HID, cols] = (cell_back * old * (1.0 - g_forget)).astype(BF16)
            delta[2 * HID : 3 * HID, cols] = (
                back_h * squash * g_out * (1.0 - g_out)
            ).astype(BF16)
            delta[3 * HID :, cols] = (back_in * (1.0 - cand * cand)).astype(BF16)
        return carry

    lax.fori_loop(1, ROWS // 2 - 1, forward, 0, unroll=UNROLL)
    for copy in halo[:2] + halo[4:]:
        copy.wait()
    for block, keep, mid, lft, rgt in ((0, keep_up, 0, 4, 5), (17, keep_down, 1, 6, 7)):
        cols = slice(block * LANES, (block + 1) * LANES)
        row = hr[mid].astype(F32)
        e[CH : 2 * CH, cols] = (row * keep).astype(BF16)
        a = jnp.where(
            lane80 == 0, pltpu.roll(hr[lft].astype(F32), 1, 1), pltpu.roll(row, 1, 1)
        )
        e[0:CH, cols] = (a * keep).astype(BF16)
        a = jnp.where(
            lane80 == LANES - 1,
            pltpu.roll(hr[rgt].astype(F32), LANES - 1, 1),
            pltpu.roll(row, LANES - 1, 1),
        )
        e[2 * CH : TAP3, cols] = (a * keep).astype(BF16)
    lax.fori_loop(0, 2, lambda c, t: forward(c * (ROWS // 2 - 1), t), 0)

    pair = []
    for dr in range(3):
        rows = TAP3 if dr < 2 else GATES
        terms = lax.dot_general(
            e[0:rows, dr * LANES : (dr + ROWS) * LANES],
            delta[:, 2 * LANES : 18 * LANES],
            (((1,), (1,)), ((), ())),
            preferred_element_type=F32,
        )
        for half in range(2):
            part = terms[:, half * LANES : (half + 1) * LANES]
            halves[half, dr * TAP3 : dr * TAP3 + rows, :] = part
        if dr == 2:
            filler = 2 * TAP3 + GATES
            halves[:, filler:PADK, :] = jnp.zeros((2, PADK - filler, LANES), F32)
            rows = PADK - 2 * TAP3
        part = pl.ds(dr * TAP3, rows)
        copy = pltpu.make_async_remote_copy(
            src_ref=halves.at[1 - core, part],
            dst_ref=pair_half.at[part],
            send_sem=c_send.at[dr],
            recv_sem=c_recv.at[dr],
            device_id=(partner, lon),
            device_id_type=MESH,
        )
        copy.start()
        pair.append(copy)

    def start_tiles(first, last):
        for n in range((nlon - 1) * first // 31, (nlon - 1) * last // 31):
            pltpu.make_async_remote_copy(
                src_ref=slots.at[peers[n]],
                dst_ref=recv.at[lon],
                send_sem=a_send,
                recv_sem=a_recv,
                device_id=(lat, peers[n]),
                device_id_type=MESH,
            ).start()


    per = PADK // nlon
    for copy in pair:
        copy.wait()

    def pack_terms(k, carry):
        rows = pl.ds(pl.multiple_of(k * per, per), per)
        wgs[k] = (halves[core, rows, :] + pair_half[rows, :]).astype(BF16)
        return carry

    lax.fori_loop(0, nlon, pack_terms, 0, unroll=4)
    rsr[lon] = wgs[lon]

    for peer in peers:
        pltpu.make_async_remote_copy(
            src_ref=wgs.at[peer],
            dst_ref=rsr.at[lon],
            send_sem=r_send,
            recv_sem=r_recv,
            device_id=(lat, peer),
            device_id_type=MESH,
        ).start()
    lane16 = lane_iota(16)
    low_of = {s: (lane16 & (16 * s)) == 0 for s in (1, 2, 4)}

    def regroup(step, carry):
        half = step // 4
        subs = pl.ds(pl.multiple_of(lax.rem(step, 4) * 16, 16), 16)
        x = [crow[half * 8 + k, subs, :] for k in range(8)]
        for s in (1, 2, 4):
            low = low_of[s]
            y = list(x)
            for k in range(8):
                if (k // s) % 2 == 0:
                    a, b = x[k], x[k + s]
                    y[k] = jnp.where(low, a, pltpu.roll(b, 16 * s, 1))
                    y[k + s] = jnp.where(low, pltpu.roll(a, LANES - 16 * s, 1), b)
            x = y
        for q in range(8):
            tiles[q, subs, row_of(half)] = x[q].astype(BF16)
        return carry

    lax.fori_loop(0, 8, regroup, 0)

    def fill(o, carry):
        slots[o] = tiles[slot_tab[o]]
        return carry

    lax.fori_loop(0, nlon, fill, 0, unroll=4)
    recv[lon] = slots[lon]

    start_tiles(BATCHES[0], BATCHES[2])

    colv_l = jnp.zeros((HID, LANES), F32)
    colv_r = jnp.zeros((HID, LANES), F32)
    for c in range(9):
        acc = jnp.zeros((TAP3, 2 * LANES), F32)
        for dr in range(3):
            start = (2 * c + 2 - dr) * LANES
            acc = acc + jnp.dot(
                w_ref[dr * TAP3 : (dr + 1) * TAP3, :],
                delta[:, start : start + 2 * LANES],
                preferred_element_type=F32,
            )
        for s in range(2):
            r = 2 * c + s
            part = acc[:, s * LANES : (s + 1) * LANES]
            s0 = part[INP:CH]
            s1 = part[CH + INP : 2 * CH]
            s2 = part[2 * CH + INP : TAP3]
            colv_l = jnp.where(lane64 == r, s0[:, 0:1], colv_l)
            colv_r = jnp.where(lane64 == r, s2[:, LANES - 1 : LANES], colv_r)
            total = (
                s1
                + jnp.where(lane64 < LANES - 1, pltpu.roll(s0, LANES - 1, 1), 0.0)
                + jnp.where(lane64 > 0, pltpu.roll(s2, 1, 1), 0.0)
            )
            if r == 0:
                gs[0] = total.astype(BF16)
            elif r == 17:
                gs[1] = total.astype(BF16)
            else:
                hg_o[r - 1] = total
    gs[2] = colv_l.astype(BF16)
    gs[3] = colv_r.astype(BF16)
    grad_plan = (
        (1, 0, (down, lon)),
        (0, 1, (up, lon)),
        (3, 2, (lat, right)),
        (2, 3, (lat, left)),
        (3, 4, (down, right)),
        (2, 5, (down, left)),
        (3, 6, (up, right)),
        (2, 7, (up, left)),
    )
    edges = []
    for src, dst, place in grad_plan:
        copy = pltpu.make_async_remote_copy(
            src_ref=gs.at[src],
            dst_ref=ge_o.at[dst],
            send_sem=g_send.at[dst],
            recv_sem=g_recv.at[dst],
            device_id=place,
            device_id_type=MESH,
        )
        copy.start()
        edges.append(copy)
    hid_o[...] = hid32[...].reshape(HID, ROWS, LANES).astype(BF16)

    def plan_work(d, carry):
        count, work = carry
        has = jnp.int32(0)
        for q in range(TILES):
            has = has + jnp.where(
                (wet[0, d * TILES + q] > 0) & (owner[0, d * TILES + q] == lon), 1, 0
            )
        work = tuple(
            work[r] + jnp.where((has > 0) & (count == r), d, 0) for r in range(CAP)
        )
        return (count + has, work)

    _, work = lax.fori_loop(
        0, nlon, plan_work, (jnp.int32(0), tuple(jnp.int32(0) for _ in range(CAP)))
    )

    drain(rsr.at[pl.ds(0, nlon - 1)], r_recv)
    lon_sum = lax.fori_loop(
        0, nlon, lambda k, t: t + rsr[k].astype(F32), jnp.zeros((per, LANES), F32), unroll=4
    )
    las[...] = lon_sum
    lar[lat // 2] = lon_sum
    across = []
    for k in range(1, places):
        copy = pltpu.make_async_remote_copy(
            src_ref=las,
            dst_ref=lar.at[lat // 2],
            send_sem=l_send.at[k],
            recv_sem=l_recv.at[k],
            device_id=(lat_peer(2 * k), lon),
            device_id_type=MESH,
        )
        copy.start()
        across.append(copy)
    start_tiles(BATCHES[2], BATCHES[3])
    for copy in across:
        copy.wait()
    total = lar[0]
    for k in range(1, places):
        total = total + lar[k]
    ags[...] = total.astype(BF16)
    ag_o[core * nlon + lon] = total.astype(BF16)

    for peer in peers + [lon]:
        for place in (lat, partner) if peer is not lon else (partner,):
            pltpu.make_async_remote_copy(
                src_ref=ags,
                dst_ref=ag_o.at[core * nlon + lon],
                send_sem=q_send,
                recv_sem=q_recv,
                device_id=(place, peer),
                device_id_type=MESH,
            ).start()
    start_tiles(BATCHES[3], BATCHES[4])
    drain(recv.at[pl.ds(0, nlon - 1)], a_recv)
    for r in range(CAP):
        cn_o[r] = recv[work[r]].astype(F32)
    for copy in edges:
        copy.wait()
    drain(ag_o.at[pl.ds(0, 2 * nlon - 1)], q_recv)
    drain(rsr.at[pl.ds(0, nlon - 1)], r_send)
    drain(ag_o.at[pl.ds(0, 2 * nlon - 1)], q_send)
    drain(recv.at[pl.ds(0, nlon - 1)], a_send)


def finish_kernel(
    nlat, nlon, scaling, hid, cg, cn, hg, ge, ag, hid_o, cn_o, hg_o, cg_o, wg_o, bg_o
):
    lat = lax.axis_index("lat")
    hid_o[...] = hid[...]
    cg_o[...] = cg[...]
    cn_o[...] = cn[...]
    lane64 = lane_iota(HID)
    keep_up = jnp.where(lat > 0, 1.0, 0.0).astype(F32)
    keep_down = jnp.where(lat < nlat - 1, 1.0, 0.0).astype(F32)
    left = ge[2].astype(F32)
    right = ge[3].astype(F32)
    for i in range(ROWS):
        row = hg[i]
        add_l = pltpu.roll(left, (LANES - 1 - i) % LANES, 1)
        add_r = pltpu.roll(right, LANES - 2 - i, 1)
        if i == 0:
            row = row + keep_up * ge[0].astype(F32)
            add_l = add_l + keep_up * pltpu.roll(ge[4].astype(F32), LANES - 17, 1)
            add_r = add_r + keep_up * pltpu.roll(ge[5].astype(F32), LANES - 18, 1)
        if i == ROWS - 1:
            row = row + keep_down * ge[1].astype(F32)
            add_l = add_l + keep_down * ge[6].astype(F32)
            add_r = add_r + keep_down * pltpu.roll(ge[7].astype(F32), LANES - 1, 1)
        row = row + jnp.where(lane64 == 0, add_l, jnp.where(lane64 == LANES - 1, add_r, 0.0))
        hg_o[pl.ds(i, HID, stride=ROWS), :] = row
    low = ag[:nlon].astype(F32).reshape(PADK, LANES) * scaling
    high = ag[nlon:].astype(F32).reshape(PADK, LANES) * scaling
    wg_o[:, :LANES] = low[: 3 * TAP3]
    wg_o[:, LANES:] = high[: 3 * TAP3]
    bg_o[:, :LANES] = low[3 * TAP3 : 3 * TAP3 + 1]
    bg_o[:, LANES:] = high[3 * TAP3 : 3 * TAP3 + 1]


def body(forcing, hidden, cell, grad_hidden, grad_cell, wet_mask, tile_owner, w_gates, b_gates):
    nlat = lax.axis_size("lat")
    nlon = lax.axis_size("lon")
    per = PADK // nlon
    anyw = pl.BlockSpec(memory_space=pltpu.HBM)
    vmem = pl.BlockSpec(memory_space=pltpu.VMEM)
    cells = HID * ROWS

    def in_hbm(x):
        return pltpu.with_memory_space_constraint(x, pltpu.HBM)

    sems = pltpu.SemaphoreType.DMA
    hid, cg, cn, hg, ge, ag = pl.pallas_call(
        functools.partial(step_kernel, nlat, nlon),
        out_shape=(
            jax.ShapeDtypeStruct((HID, ROWS, LANES), BF16),
            jax.ShapeDtypeStruct((cells, LANES), F32),
            jax.ShapeDtypeStruct((CAP, HID, 256), F32),
            jax.ShapeDtypeStruct((ROWS, HID, LANES), F32),
            jax.ShapeDtypeStruct((8, HID, LANES), BF16),
            jax.ShapeDtypeStruct((2 * nlon, per, LANES), BF16),
        ),
        in_specs=[anyw] * 9,
        out_specs=[vmem] * 6,
        scratch_shapes=[
            pltpu.VMEM((INP, ROWS, LANES), BF16),
            pltpu.VMEM((HID, ROWS, LANES), BF16),
            pltpu.VMEM((HID, ROWS, LANES), BF16),
            pltpu.VMEM((HID, ROWS, LANES), BF16),
            pltpu.VMEM((HID, ROWS, LANES), BF16),
            pltpu.VMEM((3 * TAP3, GATES), BF16),
            pltpu.VMEM((1, GATES), F32),
            pltpu.SMEM((1, nlon * TILES), jnp.int32),
            pltpu.SMEM((1, nlon * TILES), jnp.int32),
            pltpu.VMEM((INP * ROWS, LANES), F32),
            pltpu.VMEM((cells, LANES), F32),
            pltpu.VMEM((cells, LANES), F32),
            pltpu.VMEM((cells, LANES), F32),
            pltpu.VMEM((cells, LANES), F32),
            pltpu.VMEM((cells, LANES), F32),
            pltpu.VMEM((GATES, 18 * LANES), BF16),
            pltpu.VMEM((3, GATES, GATES), BF16),
            pltpu.VMEM((GATES, LANES), F32),
            pltpu.VMEM((GATES, 20 * LANES), BF16),
            pltpu.VMEM((ROWS, HID, LANES), F32),
            pltpu.VMEM((TILES, HID, 256), BF16),
            pltpu.VMEM((nlon, HID, 256), BF16),
            pltpu.VMEM((nlon, HID, 256), BF16),
            pltpu.VMEM((2, PADK, LANES), F32),
            pltpu.VMEM((PADK, LANES), F32),
            pltpu.VMEM((nlon, per, LANES), BF16),
            pltpu.VMEM((nlon, per, LANES), BF16),
            pltpu.VMEM((per, LANES), F32),
            pltpu.VMEM((nlat // 2, per, LANES), F32),
            pltpu.VMEM((per, LANES), BF16),
            pltpu.VMEM((4, CH, LANES), BF16),
            pltpu.VMEM((8, CH, LANES), BF16),
            pltpu.VMEM((4, HID, LANES), BF16),
            sems((9,)),
            sems((8,)),
            sems((8,)),
            sems((8,)),
            sems((8,)),
            sems,
            sems,
            sems((3,)),
            sems((3,)),
            sems,
            sems,
            sems((nlat // 2,)),
            sems((nlat // 2,)),
            sems,
            sems,
            pltpu.SMEM((nlon,), jnp.int32),
        ],
        compiler_params=pltpu.CompilerParams(
            collective_id=0, has_side_effects=True, vmem_limit_bytes=40 << 20
        ),
        name="step",
    )(
        in_hbm(forcing),
        in_hbm(hidden),
        in_hbm(cell),
        in_hbm(grad_hidden),
        in_hbm(grad_cell),
        in_hbm(wet_mask),
        in_hbm(tile_owner),
        in_hbm(w_gates.T),
        in_hbm(b_gates.reshape(1, GATES)),
    )
    scaling = 1.0 / math.sqrt(float(nlat * nlon * CAP * 256))
    hid, cn, hg, cg, wg, bg = pl.pallas_call(
        functools.partial(finish_kernel, nlat, nlon, scaling),
        out_shape=(
            jax.ShapeDtypeStruct((HID, ROWS, LANES), BF16),
            jax.ShapeDtypeStruct((CAP, HID, 256), F32),
            jax.ShapeDtypeStruct((cells, LANES), F32),
            jax.ShapeDtypeStruct((cells, LANES), F32),
            jax.ShapeDtypeStruct((3 * TAP3, GATES), F32),
            jax.ShapeDtypeStruct((1, GATES), F32),
        ),
        in_specs=[vmem] * 6,
        out_specs=[vmem] * 6,
        compiler_params=pltpu.CompilerParams(vmem_limit_bytes=12 << 20),
        name="finish",
    )(hid, cg, cn, hg, ge, ag)
    return (
        hid,
        cn,
        hg.reshape(HID, ROWS, LANES),
        cg.reshape(HID, ROWS, LANES),
        wg.T,
        bg.reshape(GATES),
    )


def solution(mesh):
    return jax.shard_map(
        body,
        mesh=mesh,
        in_specs=(
            P(None, "lat", "lon"),
            P(None, "lat", "lon"),
            P(None, "lat", "lon"),
            P(None, "lat", "lon"),
            P(None, "lat", "lon"),
            P("lat", None),
            P("lat", None),
            P(),
            P(),
        ),
        out_specs=(
            P(None, "lat", "lon"),
            P(("lat", "lon"), None, None),
            P(None, "lat", "lon"),
            P(None, "lat", "lon"),
            P(),
            P(),
        ),
        check_vma=False,
    )
```
